32 devices in a mesh: ctx: 4 (over y, x), exp: 8 (over z, core).
Axes of the slice: x: 2, y: 2, z: 4, core: 2. Of those that a mesh axis runs over, the one named last changes fastest.
Arguments:
- states: bfloat16 [8, 128, 2560], P('exp'), may hold values from -13 to 13
- out_grad: bfloat16 [8, 128, 2560], P('exp'), may hold values from -6 to 6
- doc_keys: bfloat16 [8, 512, 2560], P('exp', 'ctx'), may hold values from -60 to 60
- doc_values: bfloat16 [8, 512, 2560], P('exp', 'ctx'), may hold values from -18 to 18
- norm_gain: float32 [2560], replicated, may hold values from 0.5 to 1.5
- expert_ids: int32 [8, 128, 2], P('exp'), may hold values from 0 to 7, all different within a row; in each aligned block of 128 rows (0 to 127, 128 to 255, ..., all dimensions but the last counted through in order) at most 40 rows name the same one
- gate_values: float32 [8, 128, 2], P('exp'), may hold values from 0.5 to 2.5
- expert_weights: bfloat16 [8, 2048, 2, 2560], P('exp', 'ctx'), may hold values from -0.125 to 0.125
Outputs:
- states_grad: bfloat16 [8, 128, 2560], P('exp')
- keys_grad: bfloat16 [8, 512, 2560], P('exp', 'ctx')
- values_grad: bfloat16 [8, 512, 2560], P('exp', 'ctx')
- weights_grad: bfloat16 [8, 2048, 2, 2560], P('exp', 'ctx')
The draws below stay inside these ranges and needn't reach their ends.
Inputs may be any that keep to these rules, and one draw needn't show every extreme that they name: `expert_ids`: within one sequence's 128 tokens, every expert is named by at most 40 tokens.
All inputs are finite; a program needn't handle non-finite values.
Results may differ from the reference program's by a relative error of at most 0.04.
Values may be sent and summed in bfloat16 or wider, within the bound.
A program may use at most 128 MiB of HBM per device.

```python
import math
import jax
import jax.numpy as jnp
import numpy as np
from jax import lax

HEADS = 20
HEAD = 128
D = 2560
EXPERT_FF = 2048
TOP = 2
EXPERTS = 8
DEC_DEV = 128
SEQS = 8
DOC_LEN = 512
CAP = 40
N_CTX = 4


def shared_states(key):
    base = jax.random.normal(jax.random.fold_in(key, 11), (SEQS, DEC_DEV, D), jnp.float32)
    return jnp.clip(base, -4.5, 4.5)


def draw_states(key, part):
    return shared_states(key).astype(jnp.bfloat16)


def draw_doc_keys(key, part):
    noise = jax.random.normal(jax.random.fold_in(key, 23), (SEQS, DOC_LEN, D), jnp.float32)
    noise = jnp.clip(noise, -6.0, 6.0) * 2.0
    return noise.astype(jnp.bfloat16)


def steps_of(own_key, shape, cuts, low, top_value):
    level = 1.0
    for axis_at, parts in cuts:
        draws = jax.random.uniform(jax.random.fold_in(jax.random.fold_in(own_key, 6), axis_at), (parts,), jnp.float32, low / len(cuts), top_value / len(cuts))
        level = level * jnp.repeat(jnp.exp(draws), shape[axis_at] // parts).reshape((-1,) + (1,) * (len(shape) - 1 - axis_at))
    return level


def assign_block(rng, own, number, rows, number_of, top, limit, slope):
    ranking = jax.random.permutation(rng, number_of)
    heavy_load, usual = load_shares(number_of, rows * top, limit, slope, True), load_shares(number_of, rows * top, limit, slope, False)
    places = jnp.arange(number_of)

    def named(sizes, offset_by):
        used = int((sizes > 0).sum())
        fixed = max(1, used // 4)
        shifted = fixed + (places - fixed + offset_by * (used - fixed)) % max(1, number_of - fixed)
        return jnp.zeros((number_of,), jnp.int32).at[ranking[jnp.where(places < fixed, places, shifted)]].set(jnp.asarray(sizes, jnp.int32))

    sizes = jnp.where(number % 4 == 0, named(heavy_load, number // 4), named(usual, number - number // 4 - 1))
    mixed = jax.random.permutation(jax.random.fold_in(own, 3), number_of)
    source_of, receiver = mixed[0:number_of // 2 * 2:2], mixed[1:number_of // 2 * 2:2]
    room = jnp.minimum(sizes[source_of] - 1, limit - sizes[receiver]) // 2
    room = jnp.where((source_of == ranking[0]) | (receiver == ranking[0]) | (sizes[receiver] == 0), 0, jnp.maximum(room, 0))
    shifted = jax.random.randint(jax.random.fold_in(own, 4), (number_of // 2,), 0, 1 << 20) % (room + 1)
    sizes = sizes.at[source_of].add(-shifted).at[receiver].add(shifted)
    items = jnp.searchsorted(jnp.cumsum(sizes), jnp.arange(rows * top), side="right").astype(jnp.int32)
    grid = items.reshape(top, rows).T
    grid = grid[jax.random.permutation(jax.random.fold_in(own, 1), rows)]
    offset_by = jax.random.randint(jax.random.fold_in(own, 2), (rows, 1), 0, top)
    return jnp.take_along_axis(grid, (jnp.arange(top)[None, :] + offset_by) % top, axis=1)


def load_shares(number_of, total, reach, slope, full):
    loads = [(1 << 20) // math.isqrt(rank ** slope) + 1 for rank in range(1, number_of + 1)]
    largest = reach if full else min(reach, max(-(-total // number_of), total * loads[0] // sum(loads)))
    least = 1 if total - largest >= number_of - 1 else 0
    holding, surplus = [largest] + [least] * (number_of - 1), total - largest - least * (number_of - 1)
    while surplus > 0:
        candidates = [i for i in range(1, number_of) if holding[i] < largest] or [i for i in range(1, number_of) if holding[i] < reach]
        pool, remaining = sum([loads[i] for i in candidates]), surplus
        for i in candidates:
            extra = min(reach - holding[i], max(1, remaining * loads[i] // pool), surplus)
            holding[i] = holding[i] + extra
            surplus = surplus - extra
    return np.array(holding)


def bell_draw(rng, dims, scale, limit, shards=(), kind=jnp.bfloat16):
    result = scale * jax.random.normal(rng, dims, jnp.float32)
    if shards:
        result = result * steps_of(rng, dims, shards, -0.22, 0.18)
    return jnp.clip(result, -limit, limit).astype(kind)


def setup_inputs(seed: int = 0) -> dict:
    splits = jax.random.split(jax.random.key(seed), 9)
    states = draw_states(jax.random.fold_in(splits[8], 71), 0)
    out_grad = bell_draw(splits[1], (SEQS, DEC_DEV, D), 1.0, 6.0, ((0, 8),))
    doc_keys = draw_doc_keys(jax.random.fold_in(splits[8], 71), 0)
    doc_values = bell_draw(splits[3], (SEQS, DOC_LEN, D), 3.0, 18.0, ((0, 8), (1, 4)))
    norm_gain = jnp.clip(1.0 + 0.1 * jax.random.normal(splits[4], (D,), jnp.float32), 0.5, 1.5)
    expert_ids_keys = jax.random.split(jax.random.fold_in(splits[5], 1), SEQS * DEC_DEV // DEC_DEV)
    expert_ids_turns = jax.random.permutation(jax.random.fold_in(splits[5], 3), SEQS * DEC_DEV // DEC_DEV)
    expert_ids = jax.vmap(lambda own, number: assign_block(jax.random.fold_in(splits[5], 2), own, number, DEC_DEV, EXPERTS, TOP, CAP, 2))(expert_ids_keys, expert_ids_turns).reshape((SEQS, DEC_DEV, TOP))
    gate_values = jnp.clip(0.5 + 2.0 * jax.random.uniform(splits[6], (SEQS, DEC_DEV, TOP), jnp.float32) ** steps_of(splits[6], (SEQS, DEC_DEV, TOP), ((0, 8),), -0.2, 0.2), 0.5, 2.5)
    expert_weights = bell_draw(splits[7], (EXPERTS, EXPERT_FF, 2, D), D ** -0.5, 0.125, ((0, 8), (1, 4)))
    return dict(states=states, out_grad=out_grad, doc_keys=doc_keys, doc_values=doc_values, norm_gain=norm_gain, expert_ids=expert_ids, gate_values=gate_values, expert_weights=expert_weights)


EPSILON = 1e-05

def attend_back(items):
    normed, doc_keys, doc_values, upstream = items
    scale = HEAD ** (-0.5)
    queries = normed.reshape(DEC_DEV, HEADS, HEAD).astype(jnp.float32)
    key_heads = doc_keys.reshape(DOC_LEN, HEADS, HEAD).astype(jnp.float32)
    value_heads = doc_values.reshape(DOC_LEN, HEADS, HEAD).astype(jnp.float32)
    grad_heads = upstream.reshape(DEC_DEV, HEADS, HEAD).astype(jnp.float32)
    highest = lax.Precision.HIGHEST
    scores = jnp.einsum('qhd,khd->hqk', queries, key_heads, precision=highest) * scale
    peak = lax.optimization_barrier(jnp.max(scores, axis=-1, keepdims=True))
    weights = jnp.exp(scores - peak)
    probs = weights / lax.optimization_barrier(jnp.sum(weights, axis=-1, keepdims=True))
    slopes = jnp.einsum('qhd,khd->hqk', grad_heads, value_heads, precision=highest)
    delta = lax.optimization_barrier(jnp.sum(probs * slopes, axis=-1, keepdims=True))
    score_grad = (probs * (slopes - delta)).astype(jnp.bfloat16).astype(jnp.float32)
    probs_low = probs.astype(jnp.bfloat16).astype(jnp.float32)
    values_grad = jnp.einsum('hqk,qhd->khd', probs_low, grad_heads, precision=highest)
    keys_grad = jnp.einsum('hqk,qhd->khd', score_grad, queries, precision=highest) * scale
    query_grad = jnp.einsum('hqk,khd->qhd', score_grad, key_heads, precision=highest) * scale
    return (query_grad.reshape(DEC_DEV, D), keys_grad.reshape(DOC_LEN, D).astype(jnp.bfloat16), values_grad.reshape(DOC_LEN, D).astype(jnp.bfloat16))

def expert_back(normed, out_grad, expert_ids, gate_values, expert_weights):
    assigned = SEQS * DEC_DEV * TOP
    slot_total = SEQS * CAP
    group_width = EXPERT_FF // N_CTX
    flat_ids = expert_ids.reshape(assigned)
    gate_flat = gate_values.reshape(assigned).astype(jnp.float32)
    rows_all = normed.reshape(SEQS * DEC_DEV, D)
    grads_all = out_grad.reshape(SEQS * DEC_DEV, D)

    def step(carry, item):
        index, weights = item
        found = jnp.nonzero(flat_ids == index, size=slot_total, fill_value=assigned)[0].astype(jnp.int32)
        filled = found < assigned
        safe_index = jnp.minimum(found, assigned - 1)
        source = safe_index // TOP
        rows = jnp.where(filled[:, None], rows_all[source], jnp.zeros((), rows_all.dtype))
        gates = jnp.where(filled, gate_flat[safe_index], 0.0)
        douts = (gates[:, None] * grads_all[source].astype(jnp.float32)).astype(jnp.bfloat16)
        w_in = weights[:, 0, :]
        w_out = weights[:, 1, :]
        pre = jnp.dot(rows, w_in.T, preferred_element_type=jnp.float32)
        act, pull = jax.vjp(jax.nn.gelu, pre)
        act_low = act.astype(jnp.bfloat16)
        act_grad = jnp.dot(douts, w_out.T, preferred_element_type=jnp.float32)
        pre_grad = pull(act_grad)[0].astype(jnp.bfloat16)
        grad_in = jnp.dot(pre_grad.T, rows, preferred_element_type=jnp.float32)
        grad_out = jnp.dot(act_low.T, douts, preferred_element_type=jnp.float32)
        stacked = jnp.stack([grad_in, grad_out], axis=1).astype(jnp.bfloat16)
        pieces = jnp.einsum('sch,chd->scd', pre_grad.reshape(slot_total, N_CTX, group_width).astype(jnp.float32), w_in.reshape(N_CTX, group_width, D).astype(jnp.float32), precision=lax.Precision.HIGHEST)
        summed = lax.optimization_barrier(jnp.sum(pieces.astype(jnp.bfloat16).astype(jnp.float32), axis=1))
        carry = carry.at[source].add(jnp.where(filled[:, None], summed, 0.0))
        return (carry, stacked)
    start = jnp.zeros((SEQS * DEC_DEV, D), jnp.float32)
    moe_grad, weights_grad = lax.scan(step, start, (jnp.arange(EXPERTS, dtype=jnp.int32), expert_weights))
    return (moe_grad, weights_grad)

def reference(states, out_grad, doc_keys, doc_values, norm_gain, expert_ids, gate_values, expert_weights):
    inputs = states.astype(jnp.float32)
    inverse = lax.rsqrt(lax.optimization_barrier(jnp.mean(inputs * inputs, axis=-1, keepdims=True)) + EPSILON)
    unit = inputs * inverse
    normed = (unit * norm_gain).astype(jnp.bfloat16)
    query_grad, keys_grad, values_grad = lax.map(attend_back, (normed, doc_keys, doc_values, out_grad))
    moe_grad, weights_grad = expert_back(normed, out_grad, expert_ids, gate_values, expert_weights)
    total_grad = query_grad + moe_grad.reshape(SEQS, DEC_DEV, D)
    scaled = total_grad * norm_gain
    states_grad = out_grad.astype(jnp.float32) + inverse * (scaled - unit * lax.optimization_barrier(jnp.mean(scaled * unit, axis=-1, keepdims=True)))
    return (states_grad.astype(jnp.bfloat16), keys_grad, values_grad, weights_grad)
```

```python
import jax
import jax.numpy as jnp
from jax import lax
from jax.sharding import PartitionSpec as P

HEADS = 20
HEAD = 128
TOP = 2


EPSILON = 1e-05


def on_device(
    states, out_grad, doc_keys, doc_values, norm_gain, expert_ids, gate_values, expert_weights
):
    tokens = states.shape[1]
    model_width = states.shape[2]
    key_count = doc_keys.shape[1]
    scale = HEAD ** (-0.5)
    inputs = states[0].astype(jnp.float32)
    inverse = lax.rsqrt(jnp.mean(inputs * inputs, axis=-1, keepdims=True) + EPSILON)
    unit = inputs * inverse
    normed = (unit * norm_gain).astype(jnp.bfloat16)
    upstream = out_grad[0]
    queries = normed.reshape(tokens, HEADS, HEAD)
    key_heads = doc_keys[0].reshape(key_count, HEADS, HEAD)
    value_heads = doc_values[0].reshape(key_count, HEADS, HEAD)
    grad_heads = upstream.reshape(tokens, HEADS, HEAD)
    scores = (
        jnp.einsum("qhd,khd->hqk", queries, key_heads, preferred_element_type=jnp.float32) * scale
    )
    local_peak = jnp.max(scores, axis=-1)
    local_weights = jnp.exp(scores - local_peak[..., None])
    local_total = jnp.sum(local_weights, axis=-1)
    slopes = jnp.einsum("qhd,khd->hqk", grad_heads, value_heads, preferred_element_type=jnp.float32)
    local_inner = jnp.sum(local_weights * slopes, axis=-1)
    stats = lax.all_gather(jnp.stack([local_peak, local_total, local_inner]), "ctx")
    peak = jnp.max(stats[:, 0], axis=0)
    factors = jnp.exp(stats[:, 0] - peak[None])
    total = jnp.sum(stats[:, 1] * factors, axis=0)
    merged = jnp.sum(stats[:, 2] * factors, axis=0)
    delta = merged / total
    probs = jnp.exp(scores - peak[..., None]) / total[..., None]
    score_grad = (probs * (slopes - delta[..., None])).astype(jnp.bfloat16)
    probs_low = probs.astype(jnp.bfloat16)
    values_grad = jnp.einsum(
        "hqk,qhd->khd", probs_low, grad_heads, preferred_element_type=jnp.float32
    )
    keys_grad = (
        jnp.einsum("hqk,qhd->khd", score_grad, queries, preferred_element_type=jnp.float32) * scale
    )
    query_grad = (
        jnp.einsum(
            "hqk,khd->qhd", score_grad, key_heads, preferred_element_type=jnp.float32
        ).reshape(tokens, model_width)
        * scale
    )
    ctx_count = lax.axis_size("ctx")
    expert_count = lax.axis_size("exp")
    capacity = ctx_count * (
        (5 * TOP * tokens + 4 * expert_count * ctx_count - 1) // (4 * expert_count * ctx_count)
    )
    ids = expert_ids[0]
    named = ids[:, :, None] == jnp.arange(expert_count, dtype=jnp.int32)[None, None, :]
    chosen = jnp.any(named, axis=1).astype(jnp.bfloat16)
    gates = jnp.sum(jnp.where(named, gate_values[0][:, :, None], 0.0), axis=1)
    before = jnp.tri(tokens, k=-1, dtype=jnp.bfloat16)
    slot = jnp.dot(before, chosen, preferred_element_type=jnp.float32)
    slot = jnp.where(chosen > 0, slot, -1.0)
    select = slot.T[:, None, :] == jnp.arange(capacity, dtype=jnp.float32)[None, :, None]
    slot_gate = jnp.sum(jnp.where(select, gates.T[:, None, :], 0.0), axis=-1)
    select = select.astype(jnp.bfloat16).reshape(expert_count * capacity, tokens)
    me = lax.axis_index("ctx")
    share = model_width // ctx_count
    own_normed = lax.dynamic_slice_in_dim(normed, me * share, share, 1)
    own_upstream = lax.dynamic_slice_in_dim(upstream, me * share, share, 1)
    send_rows = jnp.dot(select, own_normed, preferred_element_type=jnp.float32)
    send_grads = jnp.dot(select, own_upstream, preferred_element_type=jnp.float32)
    send_grads = send_grads * slot_gate.reshape(-1, 1)
    sends = jnp.stack([send_rows, send_grads]).astype(jnp.bfloat16)
    sends = sends.reshape(2, expert_count, capacity, share)
    got = lax.all_to_all(sends, "exp", split_axis=1, concat_axis=1, tiled=True)
    slot_rows = expert_count * capacity
    got = lax.all_gather(got.reshape(2, slot_rows, share), "ctx", axis=2, tiled=True)
    rows, douts = got[0], got[1]
    w_in = expert_weights[0, :, 0, :]
    w_out = expert_weights[0, :, 1, :]
    pre = jnp.einsum("sd,hd->sh", rows, w_in, preferred_element_type=jnp.float32)
    activ, pull = jax.vjp(jax.nn.gelu, pre)
    activ_low = activ.astype(jnp.bfloat16)
    act_grad = jnp.einsum("sd,hd->sh", douts, w_out, preferred_element_type=jnp.float32)
    pre_grad = pull(act_grad)[0].astype(jnp.bfloat16)
    grad_in = jnp.einsum("sh,sd->hd", pre_grad, rows, preferred_element_type=jnp.float32)
    grad_proj = jnp.einsum("sh,sd->hd", activ_low, douts, preferred_element_type=jnp.float32)
    weights_grad = jnp.stack([grad_in, grad_proj], axis=1).astype(jnp.bfloat16)[None]
    partial_rows = jnp.einsum("sh,hd->sd", pre_grad, w_in, preferred_element_type=jnp.float32)
    partial_rows = lax.psum_scatter(
        partial_rows.astype(jnp.bfloat16), "ctx", scatter_dimension=1, tiled=True
    ).reshape(expert_count, capacity, share)
    returned = lax.all_to_all(partial_rows, "exp", split_axis=0, concat_axis=0, tiled=True)
    moe_part = jnp.einsum(
        "st,sd->td", select, returned.reshape(slot_rows, share), preferred_element_type=jnp.float32
    )
    query_part = lax.psum_scatter(
        query_grad.astype(jnp.bfloat16), "ctx", scatter_dimension=1, tiled=True
    )
    total_grad = (query_part.astype(jnp.float32) + moe_part).astype(jnp.bfloat16)
    total_grad = lax.all_gather(total_grad, "ctx", axis=1, tiled=True).astype(jnp.float32)
    scaled = total_grad * norm_gain
    states_grad = upstream.astype(jnp.float32) + inverse * (
        scaled - unit * jnp.mean(scaled * unit, axis=-1, keepdims=True)
    )
    return (
        states_grad.astype(jnp.bfloat16)[None],
        keys_grad.reshape(key_count, model_width).astype(jnp.bfloat16)[None],
        values_grad.reshape(key_count, model_width).astype(jnp.bfloat16)[None],
        weights_grad,
    )


def solution(mesh):
    return jax.shard_map(
        on_device,
        mesh=mesh,
        in_specs=(
            P("exp", None, None),
            P("exp", None, None),
            P("exp", "ctx", None),
            P("exp", "ctx", None),
            P(),
            P("exp", None, None),
            P("exp", None, None),
            P("exp", "ctx", None, None),
        ),
        out_specs=(
            P("exp", None, None),
            P("exp", "ctx", None),
            P("exp", "ctx", None),
            P("exp", "ctx", None, None),
        ),
        check_vma=False,
    )
```

```python
import functools
import jax
import jax.numpy as jnp
from jax import lax
from jax.experimental import pallas as pl
from jax.experimental.pallas import tpu as pltpu
from jax.sharding import PartitionSpec as P

HEADS = 20
HEAD = 128
TOP = 2


EPSILON = 1e-05
MESH = pl.DeviceIdType.MESH
F32 = jnp.float32
BF16 = jnp.bfloat16
VMEM_LIMIT = 60 * 1024 * 1024


def dot(a, b, ca, cb):
    return lax.dot_general(a, b, (((ca,), (cb,)), ((), ())), preferred_element_type=F32)


def head_cols(h):
    return pl.ds(pl.multiple_of(h * HEAD, HEAD), HEAD)


def front_kernel(experts, capacity, states, upstream, keys, values, gain, ids, gates, normed, sends, select, stats):
    tokens = states.shape[0]
    inputs = states[...].astype(F32)
    inverse = lax.rsqrt(jnp.mean(inputs * inputs, axis=-1, keepdims=True) + EPSILON)
    normed[...] = (inputs * inverse * gain[...]).astype(BF16)
    expert = lax.broadcasted_iota(jnp.int32, (experts, tokens), 0)
    first, second = ids[0:1, :] == expert, ids[1:2, :] == expert
    chosen = jnp.where(first | second, 1.0, 0.0)
    gate = jnp.where(first, gates[0:1, :], jnp.where(second, gates[1:2, :], 0.0))
    row = lax.broadcasted_iota(jnp.int32, (tokens, tokens), 0)
    col = lax.broadcasted_iota(jnp.int32, (tokens, tokens), 1)
    before = jnp.where(row < col, 1.0, 0.0).astype(BF16)
    slot = dot(chosen.astype(BF16), before, 1, 0)
    slot = jnp.where(chosen > 0.5, slot, -1.0)
    number = lax.broadcasted_iota(jnp.int32, (capacity, tokens), 0).astype(F32)
    for e in range(experts):
        picked = jnp.where(slot[e : e + 1, :] == number, 1.0, 0.0)
        slot_gate = jnp.sum(picked * gate[e : e + 1, :], axis=1, keepdims=True)
        picked = picked.astype(BF16)
        select[e] = picked
        sends[0, e] = dot(picked, normed[...], 1, 0).astype(BF16)
        sends[1, e] = (dot(picked, upstream[...], 1, 0) * slot_gate).astype(BF16)

    def one(h, carry):
        cols = head_cols(h)
        scores = dot(keys[:, cols], normed[:, cols], 1, 1) * HEAD ** (-0.5)
        peak = jnp.max(scores, axis=0, keepdims=True)
        weights = jnp.exp(scores - peak)
        slopes = dot(values[:, cols], upstream[:, cols], 1, 1)
        stats[0, pl.ds(h, 1), :] = peak
        stats[1, pl.ds(h, 1), :] = jnp.sum(weights, axis=0, keepdims=True)
        stats[2, pl.ds(h, 1), :] = jnp.sum(weights * slopes, axis=0, keepdims=True)
        return carry

    lax.fori_loop(0, HEADS, one, 0, unroll=4)


def entry_barrier(ctx_count, experts, c, e):
    barrier = pltpu.get_barrier_semaphore()
    for d in range(1, ctx_count):
        pl.semaphore_signal(barrier, inc=1, device_id={"ctx": lax.rem(c + d, ctx_count), "exp": e}, device_id_type=MESH)
    for d in range(1, experts):
        pl.semaphore_signal(barrier, inc=1, device_id={"ctx": c, "exp": lax.rem(e + d, experts)}, device_id_type=MESH)
    pl.semaphore_wait(barrier, ctx_count + experts - 2)


def dispatch_kernel(
    ctx_count, experts, normed, upstream, keys, values, sends, stats,
    got, keys_grad, values_grad, query_grad,
    stats_all, merged, direct_sem, forward_sem, got_sem, stats_send, stats_got,
):
    c, e = lax.axis_index("ctx"), lax.axis_index("exp")
    entry_barrier(ctx_count, experts, c, e)

    def stats_copy(d):
        peer = lax.rem(c + d, ctx_count)
        return pltpu.make_async_remote_copy(
            src_ref=stats, dst_ref=stats_all.at[ctx_count - 1 - d],
            send_sem=stats_send.at[d - 1], recv_sem=stats_got.at[ctx_count - 1 - d],
            device_id={"ctx": peer, "exp": e}, device_id_type=MESH,
        )

    def direct_copy(t, d):
        to = lax.rem(e + d, experts)
        return pltpu.make_async_remote_copy(
            src_ref=sends.at[t, to], dst_ref=got.at[t, e],
            send_sem=direct_sem.at[t, d], recv_sem=got_sem.at[t, e],
            device_id={"ctx": c, "exp": to}, device_id_type=MESH,
        )

    def forward_copy(t, s, d):
        return pltpu.make_async_remote_copy(
            src_ref=got.at[t, s], dst_ref=got.at[t, s],
            send_sem=forward_sem.at[t, s, d - 1], recv_sem=got_sem.at[t, s],
            device_id={"ctx": lax.rem(c + d, ctx_count), "exp": e}, device_id_type=MESH,
        )

    def goes(d):
        return (lax.rem(e, ctx_count) == c) | (lax.rem(e + d, experts) // 2 == e // 2)

    for d in range(1, ctx_count):
        stats_copy(d).start()
    for t in range(2):
        for d in range(1, experts):
            @pl.when(goes(d))
            def _():
                direct_copy(t, d).start()
    for t in range(2):
        got[t, e] = sends[t, e]
    for d in range(1, ctx_count):
        stats_copy(d).wait()
    peak = stats[0]
    for d in range(ctx_count - 1):
        peak = jnp.maximum(peak, stats_all[d, 0])
    factor = jnp.exp(stats[0] - peak)
    total, inner = stats[1] * factor, stats[2] * factor
    for d in range(ctx_count - 1):
        factor = jnp.exp(stats_all[d, 0] - peak)
        total = total + stats_all[d, 1] * factor
        inner = inner + stats_all[d, 2] * factor
    merged[0] = peak
    merged[1] = total
    merged[2] = inner / total

    def one(h, carry):
        cols = head_cols(h)
        k, q, g = keys[:, cols], normed[:, cols], upstream[:, cols]
        scores = dot(k, q, 1, 1) * HEAD ** (-0.5)
        probs = jnp.exp(scores - merged[0, pl.ds(h, 1), :]) / merged[1, pl.ds(h, 1), :]
        slopes = dot(values[:, cols], g, 1, 1)
        score_grad = (probs * (slopes - merged[2, pl.ds(h, 1), :])).astype(BF16)
        values_grad[:, cols] = dot(probs.astype(BF16), g, 1, 0).astype(BF16)
        keys_grad[:, cols] = (dot(score_grad, q, 1, 0) * HEAD ** (-0.5)).astype(BF16)
        query_grad[:, cols] = (dot(score_grad, k, 0, 0) * HEAD ** (-0.5)).astype(BF16)
        return carry

    lax.fori_loop(0, HEADS, one, 0)

    def got_copy(t, s):
        return pltpu.make_async_remote_copy(
            src_ref=got.at[t, s], dst_ref=got.at[t, s],
            send_sem=direct_sem.at[t, 0], recv_sem=got_sem.at[t, s],
            device_id={"ctx": c, "exp": lax.rem(e + 1, experts)}, device_id_type=MESH,
        )

    for t in range(2):
        for s in range(experts):
            @pl.when((s % ctx_count == c) & (s // 2 != e // 2))
            def _():
                got_copy(t, s).wait_recv()
                for d in range(1, ctx_count):
                    forward_copy(t, s, d).start()
    for t in range(2):
        for s in range(experts):
            @pl.when((s != e) & ((s % ctx_count != c) | (s // 2 == e // 2)))
            def _():
                got_copy(t, s).wait_recv()
    for t in range(2):
        for s in range(experts):
            @pl.when((s % ctx_count == c) & (s // 2 != e // 2))
            def _():
                for d in range(1, ctx_count):
                    forward_copy(t, s, d).wait_send()
        for d in range(1, experts):
            @pl.when(goes(d))
            def _():
                direct_copy(t, d).wait_send()


def return_kernel(
    ctx_count, experts, width, partial, query_grad, select, total,
    parts, query_parts, reduced, returned, mine, finals,
    part_send, part_got, query_send, query_got, back_send, back_got, final_send, final_got,
):
    c, e = lax.axis_index("ctx"), lax.axis_index("exp")
    tiles = partial.shape[-1] // HEAD
    entry_barrier(ctx_count, experts, c, e)

    def share(owner):
        return pl.ds(pl.multiple_of((owner * tiles // ctx_count) * HEAD, HEAD), width)

    def to_ctx(src, dst, send, recv, d):
        return pltpu.make_async_remote_copy(
            src_ref=src, dst_ref=dst.at[ctx_count - 1 - d], send_sem=send, recv_sem=recv,
            device_id={"ctx": lax.rem(c + d, ctx_count), "exp": e}, device_id_type=MESH,
        )

    def part_copy(d, o):
        peer = lax.rem(c + d, ctx_count)
        s = lax.rem(e + o, experts)
        return pltpu.make_async_remote_copy(
            src_ref=partial.at[s, :, share(peer)], dst_ref=parts.at[ctx_count - 1 - d, s],
            send_sem=part_send.at[d - 1, o], recv_sem=part_got.at[ctx_count - 1 - d, o],
            device_id={"ctx": peer, "exp": e}, device_id_type=MESH,
        )

    def query_copy(d):
        peer = lax.rem(c + d, ctx_count)
        return to_ctx(query_grad.at[:, share(peer)], query_parts, query_send.at[d - 1], query_got.at[ctx_count - 1 - d], d)

    def back_copy(o):
        s = lax.rem(e + o, experts)
        return pltpu.make_async_remote_copy(
            src_ref=reduced.at[s], dst_ref=returned.at[e],
            send_sem=back_send.at[o], recv_sem=back_got.at[experts - o],
            device_id={"ctx": c, "exp": s}, device_id_type=MESH,
        )

    def final_copy(d):
        return to_ctx(mine, finals, final_send.at[d - 1], final_got.at[ctx_count - 1 - d], d)

    order = sorted(range(experts), key=lambda o: (o == 0, abs(o - experts // 2)))
    for o in order:
        for d in range(1, ctx_count):
            part_copy(d, o).start()
    for d in range(1, ctx_count):
        query_copy(d).start()
    for o in order:
        for d in range(1, ctx_count):
            part_copy(d, o).wait()
        s = lax.rem(e + o, experts)
        summed = partial[s, :, share(c)].astype(F32)
        for d in range(ctx_count - 1):
            summed = summed + parts[d, s].astype(F32)
        if o == 0:
            returned[s] = summed.astype(BF16)
        else:
            reduced[s] = summed.astype(BF16)
            back_copy(o).start()
    summed = query_grad[:, share(c)].astype(F32)
    for d in range(1, ctx_count):
        query_copy(d).wait()
    for d in range(ctx_count - 1):
        summed = summed + query_parts[d].astype(F32)
    for o in range(1, experts):
        back_copy(o).wait()
    for s in range(experts):
        summed = summed + dot(select[s], returned[s], 0, 0)
    mine[...] = summed.astype(BF16)
    for d in range(1, ctx_count):
        final_copy(d).start()
    total[:, share(c)] = mine[...]
    for d in range(1, ctx_count):
        final_copy(d).wait()
    for d in range(1, ctx_count):
        owner = lax.rem(c + d, ctx_count)
        total[:, share(owner)] = finals[d - 1]


def on_device(
    states, out_grad, doc_keys, doc_values, norm_gain, expert_ids, gate_values, expert_weights
):
    tokens = states.shape[1]
    model_width = states.shape[2]
    key_count = doc_keys.shape[1]
    ctx_count = lax.axis_size("ctx")
    expert_count = lax.axis_size("exp")
    capacity = ctx_count * (
        (5 * TOP * tokens + 4 * expert_count * ctx_count - 1) // (4 * expert_count * ctx_count)
    )
    upstream = out_grad[0]
    vmem = pl.BlockSpec(memory_space=pltpu.VMEM)
    shape = jax.ShapeDtypeStruct
    dma = pltpu.SemaphoreType.DMA
    normed, sends, select, stats = pl.pallas_call(
        functools.partial(front_kernel, expert_count, capacity),
        out_shape=(
            shape((tokens, model_width), BF16),
            shape((2, expert_count, capacity, model_width), BF16),
            shape((expert_count, capacity, tokens), BF16),
            shape((3, HEADS, tokens), F32),
        ),
        in_specs=[vmem] * 7,
        out_specs=(vmem,) * 4,
        compiler_params=pltpu.CompilerParams(vmem_limit_bytes=VMEM_LIMIT),
    )(states[0], upstream, doc_keys[0], doc_values[0], norm_gain[None], expert_ids[0].T, gate_values[0].T)
    got, keys_grad, values_grad, query_grad = pl.pallas_call(
        functools.partial(dispatch_kernel, ctx_count, expert_count),
        out_shape=(
            shape((2, expert_count, capacity, model_width), BF16),
            shape((key_count, model_width), BF16),
            shape((key_count, model_width), BF16),
            shape((tokens, model_width), BF16),
        ),
        in_specs=[vmem] * 6,
        out_specs=(vmem,) * 4,
        scratch_shapes=[
            pltpu.VMEM((ctx_count - 1, 3, HEADS, tokens), F32),
            pltpu.VMEM((3, HEADS, tokens), F32),
            dma((2, expert_count)),
            dma((2, expert_count, ctx_count - 1)),
            dma((2, expert_count)),
            dma((ctx_count - 1,)),
            dma((ctx_count - 1,)),
        ],
        compiler_params=pltpu.CompilerParams(
            vmem_limit_bytes=VMEM_LIMIT, collective_id=0, has_side_effects=True
        ),
    )(normed, upstream, doc_keys[0], doc_values[0], sends, stats)
    slot_rows = expert_count * capacity
    rows = got[0].reshape(slot_rows, model_width)
    douts = got[1].reshape(slot_rows, model_width)
    w_in = expert_weights[0, :, 0, :]
    w_out = expert_weights[0, :, 1, :]
    pre = jnp.einsum("sd,hd->sh", rows, w_in, preferred_element_type=jnp.float32)
    activ, pull = jax.vjp(jax.nn.gelu, pre)
    activ_low = activ.astype(jnp.bfloat16)
    act_grad = jnp.einsum("sd,hd->sh", douts, w_out, preferred_element_type=jnp.float32)
    pre_grad = pull(act_grad)[0].astype(jnp.bfloat16)
    grad_in = jnp.einsum("sh,sd->hd", pre_grad, rows, preferred_element_type=jnp.float32)
    grad_proj = jnp.einsum("sh,sd->hd", activ_low, douts, preferred_element_type=jnp.float32)
    weights_grad = jnp.stack([grad_in, grad_proj], axis=1).astype(jnp.bfloat16)[None]
    partial_rows = jnp.einsum("sh,hd->sd", pre_grad, w_in, preferred_element_type=jnp.float32)
    tiles = model_width // HEAD
    width = HEAD * max(
        (c + 1) * tiles // ctx_count + ((c + 1) * tiles % ctx_count > 0) - c * tiles // ctx_count
        for c in range(ctx_count)
    )
    total_grad = pl.pallas_call(
        functools.partial(return_kernel, ctx_count, expert_count, width),
        out_shape=shape((tokens, model_width), BF16),
        in_specs=[vmem] * 3,
        out_specs=vmem,
        scratch_shapes=[
            pltpu.VMEM((ctx_count - 1, expert_count, capacity, width), BF16),
            pltpu.VMEM((ctx_count - 1, tokens, width), BF16),
            pltpu.VMEM((expert_count, capacity, width), BF16),
            pltpu.VMEM((expert_count, capacity, width), BF16),
            pltpu.VMEM((tokens, width), BF16),
            pltpu.VMEM((ctx_count - 1, tokens, width), BF16),
            dma((ctx_count - 1, expert_count)),
            dma((ctx_count - 1, expert_count)),
            dma((ctx_count - 1,)),
            dma((ctx_count - 1,)),
            dma((expert_count,)),
            dma((expert_count,)),
            dma((ctx_count - 1,)),
            dma((ctx_count - 1,)),
        ],
        compiler_params=pltpu.CompilerParams(
            vmem_limit_bytes=VMEM_LIMIT, collective_id=1, has_side_effects=True
        ),
    )(partial_rows.astype(BF16).reshape(expert_count, capacity, model_width), query_grad, select)
    total_grad = total_grad.astype(F32)
    inputs = states[0].astype(F32)
    inverse = lax.rsqrt(jnp.mean(inputs * inputs, axis=-1, keepdims=True) + EPSILON)
    unit = inputs * inverse
    scaled = total_grad * norm_gain
    states_grad = upstream.astype(jnp.float32) + inverse * (
        scaled - unit * jnp.mean(scaled * unit, axis=-1, keepdims=True)
    )
    return (
        states_grad.astype(jnp.bfloat16)[None],
        keys_grad[None],
        values_grad[None],
        weights_grad,
    )


def solution(mesh):
    return jax.shard_map(
        on_device,
        mesh=mesh,
        in_specs=(
            P("exp", None, None),
            P("exp", None, None),
            P("exp", "ctx", None),
            P("exp", "ctx", None),
            P(),
            P("exp", None, None),
            P("exp", None, None),
            P("exp", "ctx", None, None),
        ),
        out_specs=(
            P("exp", None, None),
            P("exp", "ctx", None),
            P("exp", "ctx", None),
            P("exp", "ctx", None, None),
        ),
        check_vma=False,
    )
```

```python
import functools
import jax
import jax.numpy as jnp
from jax import lax
from jax.experimental import pallas as pl
from jax.experimental.pallas import tpu as pltpu
from jax.sharding import PartitionSpec as P

HEADS = 20
HEAD = 128
TOP = 2


EPSILON = 1e-05
MESH = pl.DeviceIdType.MESH
F32 = jnp.float32
BF16 = jnp.bfloat16
VMEM_LIMIT = 60 * 1024 * 1024


def dot(a, b, ca, cb):
    return lax.dot_general(a, b, (((ca,), (cb,)), ((), ())), preferred_element_type=F32)


def head_cols(h):
    return pl.ds(pl.multiple_of(h * HEAD, HEAD), HEAD)


def front_kernel(experts, capacity, states, upstream, keys, values, gain, ids, gates, normed, sends, select, stats):
    tokens = states.shape[0]
    inputs = states[...].astype(F32)
    inverse = lax.rsqrt(jnp.mean(inputs * inputs, axis=-1, keepdims=True) + EPSILON)
    normed[...] = (inputs * inverse * gain[...]).astype(BF16)
    expert = lax.broadcasted_iota(jnp.int32, (experts, tokens), 0)
    first, second = ids[0:1, :] == expert, ids[1:2, :] == expert
    chosen = jnp.where(first | second, 1.0, 0.0)
    gate = jnp.where(first, gates[0:1, :], jnp.where(second, gates[1:2, :], 0.0))
    row = lax.broadcasted_iota(jnp.int32, (tokens, tokens), 0)
    col = lax.broadcasted_iota(jnp.int32, (tokens, tokens), 1)
    before = jnp.where(row < col, 1.0, 0.0).astype(BF16)
    slot = dot(chosen.astype(BF16), before, 1, 0)
    slot = jnp.where(chosen > 0.5, slot, -1.0)
    number = lax.broadcasted_iota(jnp.int32, (capacity, tokens), 0).astype(F32)
    for e in range(experts):
        picked = jnp.where(slot[e : e + 1, :] == number, 1.0, 0.0)
        slot_gate = jnp.sum(picked * gate[e : e + 1, :], axis=1, keepdims=True)
        picked = picked.astype(BF16)
        select[e] = picked
        sends[0, e] = dot(picked, normed[...], 1, 0).astype(BF16)
        sends[1, e] = (dot(picked, upstream[...], 1, 0) * slot_gate).astype(BF16)

    def one(h, carry):
        cols = head_cols(h)
        scores = dot(keys[:, cols], normed[:, cols], 1, 1) * HEAD ** (-0.5)
        peak = jnp.max(scores, axis=0, keepdims=True)
        weights = jnp.exp(scores - peak)
        slopes = dot(values[:, cols], upstream[:, cols], 1, 1)
        stats[0, pl.ds(h, 1), :] = peak
        stats[1, pl.ds(h, 1), :] = jnp.sum(weights, axis=0, keepdims=True)
        stats[2, pl.ds(h, 1), :] = jnp.sum(weights * slopes, axis=0, keepdims=True)
        return carry

    lax.fori_loop(0, HEADS, one, 0, unroll=4)


def entry_barrier(ctx_count, experts, c, e):
    barrier = pltpu.get_barrier_semaphore()
    for d in range(1, ctx_count):
        pl.semaphore_signal(barrier, inc=1, device_id={"ctx": lax.rem(c + d, ctx_count), "exp": e}, device_id_type=MESH)
    for d in range(1, experts):
        pl.semaphore_signal(barrier, inc=1, device_id={"ctx": c, "exp": lax.rem(e + d, experts)}, device_id_type=MESH)
    pl.semaphore_wait(barrier, ctx_count + experts - 2)


def dispatch_kernel(
    ctx_count, experts, normed, upstream, keys, values, sends, stats, weights,
    got, keys_grad, values_grad, query_grad, w_in, w_out,
    stats_all, merged, direct_sem, forward_sem, got_sem, stats_send, stats_got,
):
    c, e = lax.axis_index("ctx"), lax.axis_index("exp")
    entry_barrier(ctx_count, experts, c, e)

    def stats_copy(d):
        peer = lax.rem(c + d, ctx_count)
        return pltpu.make_async_remote_copy(
            src_ref=stats, dst_ref=stats_all.at[ctx_count - 1 - d],
            send_sem=stats_send.at[d - 1], recv_sem=stats_got.at[ctx_count - 1 - d],
            device_id={"ctx": peer, "exp": e}, device_id_type=MESH,
        )

    def direct_copy(t, d):
        to = lax.rem(e + d, experts)
        return pltpu.make_async_remote_copy(
            src_ref=sends.at[t, to], dst_ref=got.at[t, e],
            send_sem=direct_sem.at[t, d], recv_sem=got_sem.at[t, e],
            device_id={"ctx": c, "exp": to}, device_id_type=MESH,
        )

    def forward_copy(t, s, d):
        return pltpu.make_async_remote_copy(
            src_ref=got.at[t, s], dst_ref=got.at[t, s],
            send_sem=forward_sem.at[t, s, d - 1], recv_sem=got_sem.at[t, s],
            device_id={"ctx": lax.rem(c + d, ctx_count), "exp": e}, device_id_type=MESH,
        )

    def carries(t, s):
        return lax.rem(s + t * (ctx_count // 2), ctx_count) == c

    def goes(t, d):
        return carries(t, e) | (lax.rem(e + d, experts) // 2 == e // 2)

    for d in range(1, ctx_count):
        stats_copy(d).start()
    for t in range(2):
        for d in range(1, experts):
            @pl.when(goes(t, d))
            def _():
                direct_copy(t, d).start()
    for t in range(2):
        got[t, e] = sends[t, e]
    for d in range(1, ctx_count):
        stats_copy(d).wait()
    peak = stats[0]
    for d in range(ctx_count - 1):
        peak = jnp.maximum(peak, stats_all[d, 0])
    factor = jnp.exp(stats[0] - peak)
    total, inner = stats[1] * factor, stats[2] * factor
    for d in range(ctx_count - 1):
        factor = jnp.exp(stats_all[d, 0] - peak)
        total = total + stats_all[d, 1] * factor
        inner = inner + stats_all[d, 2] * factor
    merged[0] = peak
    merged[1] = total
    merged[2] = inner / total

    def one(h, carry):
        cols = head_cols(h)
        k, q, g = keys[:, cols], normed[:, cols], upstream[:, cols]
        scores = dot(k, q, 1, 1) * HEAD ** (-0.5)
        probs = jnp.exp(scores - merged[0, pl.ds(h, 1), :]) / merged[1, pl.ds(h, 1), :]
        slopes = dot(values[:, cols], g, 1, 1)
        score_grad = (probs * (slopes - merged[2, pl.ds(h, 1), :])).astype(BF16)
        values_grad[:, cols] = dot(probs.astype(BF16), g, 1, 0).astype(BF16)
        keys_grad[:, cols] = (dot(score_grad, q, 1, 0) * HEAD ** (-0.5)).astype(BF16)
        query_grad[:, cols] = (dot(score_grad, k, 0, 0) * HEAD ** (-0.5)).astype(BF16)
        return carry

    lax.fori_loop(0, HEADS // 4, one, 0)

    def got_copy(t, s):
        return pltpu.make_async_remote_copy(
            src_ref=got.at[t, s], dst_ref=got.at[t, s],
            send_sem=direct_sem.at[t, 0], recv_sem=got_sem.at[t, s],
            device_id={"ctx": c, "exp": lax.rem(e + 1, experts)}, device_id_type=MESH,
        )

    for t in range(2):
        for s in range(experts):
            @pl.when(carries(t, s) & (s // 2 != e // 2))
            def _():
                got_copy(t, s).wait_recv()
                for d in range(1, ctx_count):
                    forward_copy(t, s, d).start()
        if t == 0:
            lax.fori_loop(HEADS // 4, HEADS // 2, one, 0)
    lax.fori_loop(HEADS // 2, HEADS, one, 0)
    chunk = 64

    def split(i, carry):
        at = pl.ds(pl.multiple_of(i * chunk, chunk), chunk)
        w_in[at, :] = weights[at, 0, :]
        w_out[at, :] = weights[at, 1, :]
        return carry

    lax.fori_loop(0, weights.shape[0] // chunk, split, 0)
    for t in range(2):
        for s in range(experts):
            @pl.when((s != e) & (jnp.logical_not(carries(t, s)) | (s // 2 == e // 2)))
            def _():
                got_copy(t, s).wait_recv()
    for t in range(2):
        for s in range(experts):
            @pl.when(carries(t, s) & (s // 2 != e // 2))
            def _():
                for d in range(1, ctx_count):
                    forward_copy(t, s, d).wait_send()
        for d in range(1, experts):
            @pl.when(goes(t, d))
            def _():
                direct_copy(t, d).wait_send()


def weights_kernel(pre_grad, activ, rows, douts, grad):
    grad[:, 0, :] = dot(pre_grad[...], rows[...], 0, 0).astype(BF16)
    grad[:, 1, :] = dot(activ[...], douts[...], 0, 0).astype(BF16)


def return_kernel(
    ctx_count, experts, width, partial, query_grad, select, total,
    parts, query_parts, reduced, returned, mine, finals,
    part_send, part_got, query_send, query_got, back_send, back_got, final_send, final_got,
):
    c, e = lax.axis_index("ctx"), lax.axis_index("exp")
    tiles = partial.shape[-1] // HEAD
    entry_barrier(ctx_count, experts, c, e)

    def share(owner):
        return pl.ds(pl.multiple_of((owner * tiles // ctx_count) * HEAD, HEAD), width)

    def to_ctx(src, dst, send, recv, d):
        return pltpu.make_async_remote_copy(
            src_ref=src, dst_ref=dst.at[ctx_count - 1 - d], send_sem=send, recv_sem=recv,
            device_id={"ctx": lax.rem(c + d, ctx_count), "exp": e}, device_id_type=MESH,
        )

    def part_copy(d, o):
        peer = lax.rem(c + d, ctx_count)
        s = lax.rem(e + o, experts)
        return pltpu.make_async_remote_copy(
            src_ref=partial.at[s, :, share(peer)], dst_ref=parts.at[ctx_count - 1 - d, s],
            send_sem=part_send.at[d - 1, o], recv_sem=part_got.at[ctx_count - 1 - d, o],
            device_id={"ctx": peer, "exp": e}, device_id_type=MESH,
        )

    def query_copy(d):
        peer = lax.rem(c + d, ctx_count)
        return to_ctx(query_grad.at[:, share(peer)], query_parts, query_send.at[d - 1], query_got.at[ctx_count - 1 - d], d)

    def back_copy(o):
        s = lax.rem(e + o, experts)
        return pltpu.make_async_remote_copy(
            src_ref=reduced.at[s], dst_ref=returned.at[e],
            send_sem=back_send.at[o], recv_sem=back_got.at[experts - o],
            device_id={"ctx": c, "exp": s}, device_id_type=MESH,
        )

    def final_copy(d):
        return to_ctx(mine, finals, final_send.at[d - 1], final_got.at[ctx_count - 1 - d], d)

    order = sorted(range(experts), key=lambda o: (o == 0, abs(o - experts // 2)))
    for o in order:
        for d in range(1, ctx_count):
            part_copy(d, o).start()
    for d in range(1, ctx_count):
        query_copy(d).start()
    for o in order:
        for d in range(1, ctx_count):
            part_copy(d, o).wait()
        s = lax.rem(e + o, experts)
        summed = partial[s, :, share(c)].astype(F32)
        for d in range(ctx_count - 1):
            summed = summed + parts[d, s].astype(F32)
        if o == 0:
            returned[s] = summed.astype(BF16)
        else:
            reduced[s] = summed.astype(BF16)
            back_copy(o).start()
    summed = query_grad[:, share(c)].astype(F32)
    for d in range(1, ctx_count):
        query_copy(d).wait()
    for d in range(ctx_count - 1):
        summed = summed + query_parts[d].astype(F32)
    for o in range(1, experts):
        back_copy(o).wait()
    for s in range(experts):
        summed = summed + dot(select[s], returned[s], 0, 0)
    mine[...] = summed.astype(BF16)
    for d in range(1, ctx_count):
        final_copy(d).start()
    total[:, share(c)] = mine[...]
    for d in range(1, ctx_count):
        final_copy(d).wait()
    for d in range(1, ctx_count):
        owner = lax.rem(c + d, ctx_count)
        total[:, share(owner)] = finals[d - 1]


def on_device(
    states, out_grad, doc_keys, doc_values, norm_gain, expert_ids, gate_values, expert_weights
):
    tokens = states.shape[1]
    model_width = states.shape[2]
    key_count = doc_keys.shape[1]
    ctx_count = lax.axis_size("ctx")
    expert_count = lax.axis_size("exp")
    capacity = ctx_count * (
        (5 * TOP * tokens + 4 * expert_count * ctx_count - 1) // (4 * expert_count * ctx_count)
    )
    upstream = out_grad[0]
    hidden = expert_weights.shape[1]
    vmem = pl.BlockSpec(memory_space=pltpu.VMEM)
    shape = jax.ShapeDtypeStruct
    dma = pltpu.SemaphoreType.DMA
    normed, sends, select, stats = pl.pallas_call(
        functools.partial(front_kernel, expert_count, capacity),
        out_shape=(
            shape((tokens, model_width), BF16),
            shape((2, expert_count, capacity, model_width), BF16),
            shape((expert_count, capacity, tokens), BF16),
            shape((3, HEADS, tokens), F32),
        ),
        in_specs=[vmem] * 7,
        out_specs=(vmem,) * 4,
        compiler_params=pltpu.CompilerParams(vmem_limit_bytes=VMEM_LIMIT),
    )(states[0], upstream, doc_keys[0], doc_values[0], norm_gain[None], expert_ids[0].T, gate_values[0].T)
    got, keys_grad, values_grad, query_grad, w_in, w_out = pl.pallas_call(
        functools.partial(dispatch_kernel, ctx_count, expert_count),
        out_shape=(
            shape((2, expert_count, capacity, model_width), BF16),
            shape((key_count, model_width), BF16),
            shape((key_count, model_width), BF16),
            shape((tokens, model_width), BF16),
            shape((hidden, model_width), BF16),
            shape((hidden, model_width), BF16),
        ),
        in_specs=[vmem] * 7,
        out_specs=(vmem,) * 6,
        scratch_shapes=[
            pltpu.VMEM((ctx_count - 1, 3, HEADS, tokens), F32),
            pltpu.VMEM((3, HEADS, tokens), F32),
            dma((2, expert_count)),
            dma((2, expert_count, ctx_count - 1)),
            dma((2, expert_count)),
            dma((ctx_count - 1,)),
            dma((ctx_count - 1,)),
        ],
        compiler_params=pltpu.CompilerParams(
            vmem_limit_bytes=VMEM_LIMIT, collective_id=0, has_side_effects=True
        ),
    )(normed, upstream, doc_keys[0], doc_values[0], sends, stats, expert_weights[0])
    slot_rows = expert_count * capacity
    rows = got[0].reshape(slot_rows, model_width)
    douts = got[1].reshape(slot_rows, model_width)
    pre = jnp.einsum("sd,hd->sh", rows, w_in, preferred_element_type=jnp.float32)
    activ, pull = jax.vjp(jax.nn.gelu, pre)
    activ_low = activ.astype(jnp.bfloat16)
    act_grad = jnp.einsum("sd,hd->sh", douts, w_out, preferred_element_type=jnp.float32)
    pre_grad = pull(act_grad)[0].astype(jnp.bfloat16)
    block = min(hidden, 128)
    hidden_spec = pl.BlockSpec((slot_rows, block), lambda i: (0, i))
    rows_spec = pl.BlockSpec((slot_rows, model_width), lambda i: (0, 0))
    weights_grad = pl.pallas_call(
        weights_kernel,
        grid=(hidden // block,),
        out_shape=shape((hidden, 2, model_width), BF16),
        in_specs=[hidden_spec, hidden_spec, rows_spec, rows_spec],
        out_specs=pl.BlockSpec((block, 2, model_width), lambda i: (i, 0, 0)),
        compiler_params=pltpu.CompilerParams(vmem_limit_bytes=VMEM_LIMIT),
    )(pre_grad, activ_low, rows, douts)[None]
    partial_rows = jnp.einsum("sh,hd->sd", pre_grad, w_in, preferred_element_type=jnp.float32)
    tiles = model_width // HEAD
    width = HEAD * max(
        (c + 1) * tiles // ctx_count + ((c + 1) * tiles % ctx_count > 0) - c * tiles // ctx_count
        for c in range(ctx_count)
    )
    total_grad = pl.pallas_call(
        functools.partial(return_kernel, ctx_count, expert_count, width),
        out_shape=shape((tokens, model_width), BF16),
        in_specs=[vmem] * 3,
        out_specs=vmem,
        scratch_shapes=[
            pltpu.VMEM((ctx_count - 1, expert_count, capacity, width), BF16),
            pltpu.VMEM((ctx_count - 1, tokens, width), BF16),
            pltpu.VMEM((expert_count, capacity, width), BF16),
            pltpu.VMEM((expert_count, capacity, width), BF16),
            pltpu.VMEM((tokens, width), BF16),
            pltpu.VMEM((ctx_count - 1, tokens, width), BF16),
            dma((ctx_count - 1, expert_count)),
            dma((ctx_count - 1, expert_count)),
            dma((ctx_count - 1,)),
            dma((ctx_count - 1,)),
            dma((expert_count,)),
            dma((expert_count,)),
            dma((ctx_count - 1,)),
            dma((ctx_count - 1,)),
        ],
        compiler_params=pltpu.CompilerParams(
            vmem_limit_bytes=VMEM_LIMIT, collective_id=1, has_side_effects=True
        ),
    )(partial_rows.astype(BF16).reshape(expert_count, capacity, model_width), query_grad, select)
    total_grad = total_grad.astype(F32)
    inputs = states[0].astype(F32)
    inverse = lax.rsqrt(jnp.mean(inputs * inputs, axis=-1, keepdims=True) + EPSILON)
    unit = inputs * inverse
    scaled = total_grad * norm_gain
    states_grad = upstream.astype(jnp.float32) + inverse * (
        scaled - unit * jnp.mean(scaled * unit, axis=-1, keepdims=True)
    )
    return (
        states_grad.astype(jnp.bfloat16)[None],
        keys_grad[None],
        values_grad[None],
        weights_grad,
    )


def solution(mesh):
    return jax.shard_map(
        on_device,
        mesh=mesh,
        in_specs=(
            P("exp", None, None),
            P("exp", None, None),
            P("exp", "ctx", None),
            P("exp", "ctx", None),
            P(),
            P("exp", None, None),
            P("exp", None, None),
            P("exp", "ctx", None, None),
        ),
        out_specs=(
            P("exp", None, None),
            P("exp", "ctx", None),
            P("exp", "ctx", None),
            P("exp", "ctx", None, None),
        ),
        check_vma=False,
    )
```

```python
import functools
import jax
import jax.numpy as jnp
from jax import lax
from jax.experimental import pallas as pl
from jax.experimental.pallas import tpu as pltpu
from jax.sharding import PartitionSpec as P

HEADS = 20
HEAD = 128
TOP = 2


EPSILON = 1e-05
MESH = pl.DeviceIdType.MESH
F32 = jnp.float32
BF16 = jnp.bfloat16
VMEM_LIMIT = 60 * 1024 * 1024


def dot(a, b, ca, cb):
    return lax.dot_general(a, b, (((ca,), (cb,)), ((), ())), preferred_element_type=F32)


def head_cols(h):
    return pl.ds(pl.multiple_of(h * HEAD, HEAD), HEAD)


def front_kernel(experts, capacity, states, upstream, gain, ids, gates, normed, sends, select):
    tokens = states.shape[0]
    inputs = states[...].astype(F32)
    inverse = lax.rsqrt(jnp.mean(inputs * inputs, axis=-1, keepdims=True) + EPSILON)
    normed[...] = (inputs * inverse * gain[...][None]).astype(BF16)
    expert = lax.broadcasted_iota(jnp.int32, (experts, tokens), 0)
    first, second = ids[0:1, :] == expert, ids[1:2, :] == expert
    chosen = jnp.where(first | second, 1.0, 0.0)
    gate = jnp.where(first, gates[0:1, :], jnp.where(second, gates[1:2, :], 0.0))
    row = lax.broadcasted_iota(jnp.int32, (tokens, tokens), 0)
    col = lax.broadcasted_iota(jnp.int32, (tokens, tokens), 1)
    before = jnp.where(row < col, 1.0, 0.0).astype(BF16)
    slot = dot(chosen.astype(BF16), before, 1, 0)
    slot = jnp.where(chosen > 0.5, slot, -1.0)
    number = lax.broadcasted_iota(jnp.int32, (capacity, tokens), 0).astype(F32)
    for e in range(experts):
        picked = jnp.where(slot[e : e + 1, :] == number, 1.0, 0.0)
        slot_gate = jnp.sum(picked * gate[e : e + 1, :], axis=1, keepdims=True)
        picked = picked.astype(BF16)
        select[e] = picked
        sends[0, e] = dot(picked, normed[...], 1, 0).astype(BF16)
        sends[1, e] = (dot(picked, upstream[...], 1, 0) * slot_gate).astype(BF16)


def entry_barrier(ctx_count, experts, c, e):
    barrier = pltpu.get_barrier_semaphore()
    for d in range(1, ctx_count):
        pl.semaphore_signal(barrier, inc=1, device_id={"ctx": lax.rem(c + d, ctx_count), "exp": e}, device_id_type=MESH)
    for d in range(1, experts):
        pl.semaphore_signal(barrier, inc=1, device_id={"ctx": c, "exp": lax.rem(e + d, experts)}, device_id_type=MESH)
    pl.semaphore_wait(barrier, ctx_count + experts - 2)


def dispatch_kernel(
    ctx_count, experts, normed, upstream, keys, values, sends, weights,
    got_rows, got_grads, keys_grad, values_grad, query_grad, w_in, w_out,
    stats, stats_all, merged, direct_sem, forward_sem, got_sem, stats_send, stats_got,
):
    c, e = lax.axis_index("ctx"), lax.axis_index("exp")
    got = (got_rows, got_grads)
    entry_barrier(ctx_count, experts, c, e)

    def stats_copy(d):
        peer = lax.rem(c + d, ctx_count)
        return pltpu.make_async_remote_copy(
            src_ref=stats, dst_ref=stats_all.at[ctx_count - 1 - d],
            send_sem=stats_send.at[d - 1], recv_sem=stats_got.at[ctx_count - 1 - d],
            device_id={"ctx": peer, "exp": e}, device_id_type=MESH,
        )

    def direct_copy(t, d):
        to = lax.rem(e + d, experts)
        return pltpu.make_async_remote_copy(
            src_ref=sends.at[t, to], dst_ref=got[t].at[e],
            send_sem=direct_sem.at[t, d], recv_sem=got_sem.at[t, e],
            device_id={"ctx": c, "exp": to}, device_id_type=MESH,
        )

    def forward_copy(t, s, d):
        return pltpu.make_async_remote_copy(
            src_ref=got[t].at[s], dst_ref=got[t].at[s],
            send_sem=forward_sem.at[t, s, d - 1], recv_sem=got_sem.at[t, s],
            device_id={"ctx": lax.rem(c + d, ctx_count), "exp": e}, device_id_type=MESH,
        )

    def carries(t, s):
        return lax.rem(s + t * (ctx_count // 2), ctx_count) == c

    def goes(t, d):
        return carries(t, e) | (lax.rem(e + d, experts) // 2 == e // 2)

    for t in range(2):
        for d in range(1, experts):
            @pl.when(goes(t, d))
            def _():
                direct_copy(t, d).start()

    def local(h, carry):
        cols = head_cols(h)
        scores = dot(keys[:, cols], normed[:, cols], 1, 1) * HEAD ** (-0.5)
        peak = jnp.max(scores, axis=0, keepdims=True)
        weight = jnp.exp(scores - peak)
        slopes = dot(values[:, cols], upstream[:, cols], 1, 1)
        stats[0, pl.ds(h, 1), :] = peak
        stats[1, pl.ds(h, 1), :] = jnp.sum(weight, axis=0, keepdims=True)
        stats[2, pl.ds(h, 1), :] = jnp.sum(weight * slopes, axis=0, keepdims=True)
        return carry

    lax.fori_loop(0, HEADS, local, 0, unroll=4)
    for t in range(2):
        got[t][e] = sends[t, e]
    for d in range(1, ctx_count):
        stats_copy(d).start()
    for d in range(1, ctx_count):
        stats_copy(d).wait()
    peak = stats[0]
    for d in range(ctx_count - 1):
        peak = jnp.maximum(peak, stats_all[d, 0])
    factor = jnp.exp(stats[0] - peak)
    total, inner = stats[1] * factor, stats[2] * factor
    for d in range(ctx_count - 1):
        factor = jnp.exp(stats_all[d, 0] - peak)
        total = total + stats_all[d, 1] * factor
        inner = inner + stats_all[d, 2] * factor
    merged[0] = peak
    merged[1] = total
    merged[2] = inner / total

    def one(h, carry):
        cols = head_cols(h)
        k, q, g = keys[:, cols], normed[:, cols], upstream[:, cols]
        scores = dot(k, q, 1, 1) * HEAD ** (-0.5)
        probs = jnp.exp(scores - merged[0, pl.ds(h, 1), :]) / merged[1, pl.ds(h, 1), :]
        slopes = dot(values[:, cols], g, 1, 1)
        score_grad = (probs * (slopes - merged[2, pl.ds(h, 1), :])).astype(BF16)
        values_grad[:, cols] = dot(probs.astype(BF16), g, 1, 0).astype(BF16)
        keys_grad[:, cols] = (dot(score_grad, q, 1, 0) * HEAD ** (-0.5)).astype(BF16)
        query_grad[:, cols] = (dot(score_grad, k, 0, 0) * HEAD ** (-0.5)).astype(BF16)
        return carry

    lax.fori_loop(0, HEADS // 4, one, 0)

    def got_copy(t, s):
        return pltpu.make_async_remote_copy(
            src_ref=got[t].at[s], dst_ref=got[t].at[s],
            send_sem=direct_sem.at[t, 0], recv_sem=got_sem.at[t, s],
            device_id={"ctx": c, "exp": lax.rem(e + 1, experts)}, device_id_type=MESH,
        )

    for t in range(2):
        for s in range(experts):
            @pl.when(carries(t, s) & (s // 2 != e // 2))
            def _():
                got_copy(t, s).wait_recv()
                for d in range(1, ctx_count):
                    forward_copy(t, s, d).start()
        if t == 0:
            lax.fori_loop(HEADS // 4, HEADS // 2, one, 0)
    lax.fori_loop(HEADS // 2, HEADS, one, 0)
    chunk = 64

    def split(i, carry):
        at = pl.ds(pl.multiple_of(i * chunk, chunk), chunk)
        w_in[at, :] = weights[at, 0, :]
        w_out[at, :] = weights[at, 1, :]
        return carry

    lax.fori_loop(0, weights.shape[0] // chunk, split, 0)
    for t in range(2):
        for s in range(experts):
            @pl.when((s != e) & (jnp.logical_not(carries(t, s)) | (s // 2 == e // 2)))
            def _():
                got_copy(t, s).wait_recv()
    for t in range(2):
        for s in range(experts):
            @pl.when(carries(t, s) & (s // 2 != e // 2))
            def _():
                for d in range(1, ctx_count):
                    forward_copy(t, s, d).wait_send()
        for d in range(1, experts):
            @pl.when(goes(t, d))
            def _():
                direct_copy(t, d).wait_send()


def weights_kernel(pre_grad, activ, rows, douts, grad):
    grad[:, 0, :] = dot(pre_grad[...], rows[...], 0, 0).astype(BF16)
    grad[:, 1, :] = dot(activ[...], douts[...], 0, 0).astype(BF16)


def return_kernel(
    ctx_count, experts, width, partial, query_grad, select, total,
    parts, query_parts, reduced, returned, mine, finals,
    part_send, part_got, query_send, query_got, back_send, back_got, final_send, final_got,
):
    c, e = lax.axis_index("ctx"), lax.axis_index("exp")
    tiles = partial.shape[-1] // HEAD
    entry_barrier(ctx_count, experts, c, e)

    def share(owner):
        return pl.ds(pl.multiple_of((owner * tiles // ctx_count) * HEAD, HEAD), width)

    def to_ctx(src, dst, send, recv, d):
        return pltpu.make_async_remote_copy(
            src_ref=src, dst_ref=dst.at[ctx_count - 1 - d], send_sem=send, recv_sem=recv,
            device_id={"ctx": lax.rem(c + d, ctx_count), "exp": e}, device_id_type=MESH,
        )

    def part_copy(d, o):
        peer = lax.rem(c + d, ctx_count)
        s = lax.rem(e + o, experts)
        return pltpu.make_async_remote_copy(
            src_ref=partial.at[s, :, share(peer)], dst_ref=parts.at[ctx_count - 1 - d, s],
            send_sem=part_send.at[d - 1, o], recv_sem=part_got.at[ctx_count - 1 - d, o],
            device_id={"ctx": peer, "exp": e}, device_id_type=MESH,
        )

    def query_copy(d):
        peer = lax.rem(c + d, ctx_count)
        return to_ctx(query_grad.at[:, share(peer)], query_parts, query_send.at[d - 1], query_got.at[ctx_count - 1 - d], d)

    def back_copy(o):
        s = lax.rem(e + o, experts)
        return pltpu.make_async_remote_copy(
            src_ref=reduced.at[s], dst_ref=returned.at[e],
            send_sem=back_send.at[o], recv_sem=back_got.at[experts - o],
            device_id={"ctx": c, "exp": s}, device_id_type=MESH,
        )

    def final_copy(d):
        return to_ctx(mine, finals, final_send.at[d - 1], final_got.at[ctx_count - 1 - d], d)

    order = sorted(range(experts), key=lambda o: (o == 0, abs(o - experts // 2)))
    for o in order:
        for d in range(1, ctx_count):
            part_copy(d, o).start()
    for d in range(1, ctx_count):
        query_copy(d).start()
    for o in order:
        for d in range(1, ctx_count):
            part_copy(d, o).wait()
        s = lax.rem(e + o, experts)
        summed = partial[s, :, share(c)].astype(F32)
        for d in range(ctx_count - 1):
            summed = summed + parts[d, s].astype(F32)
        if o == 0:
            returned[s] = summed.astype(BF16)
        else:
            reduced[s] = summed.astype(BF16)
            back_copy(o).start()
    summed = query_grad[:, share(c)].astype(F32)
    for d in range(1, ctx_count):
        query_copy(d).wait()
    for d in range(ctx_count - 1):
        summed = summed + query_parts[d].astype(F32)
    for o in range(1, experts):
        back_copy(o).wait()
    for s in range(experts):
        summed = summed + dot(select[s], returned[s], 0, 0)
    mine[...] = summed.astype(BF16)
    for d in range(1, ctx_count):
        final_copy(d).start()
    total[:, share(c)] = mine[...]
    for d in range(1, ctx_count):
        final_copy(d).wait()
    for d in range(1, ctx_count):
        owner = lax.rem(c + d, ctx_count)
        total[:, share(owner)] = finals[d - 1]


def on_device(
    states, out_grad, doc_keys, doc_values, norm_gain, expert_ids, gate_values, expert_weights
):
    tokens = states.shape[1]
    model_width = states.shape[2]
    key_count = doc_keys.shape[1]
    ctx_count = lax.axis_size("ctx")
    expert_count = lax.axis_size("exp")
    capacity = ctx_count * (
        (5 * TOP * tokens + 4 * expert_count * ctx_count - 1) // (4 * expert_count * ctx_count)
    )
    upstream = out_grad[0]
    hidden = expert_weights.shape[1]
    vmem = pl.BlockSpec(memory_space=pltpu.VMEM)
    shape = jax.ShapeDtypeStruct
    dma = pltpu.SemaphoreType.DMA
    normed, sends, select = pl.pallas_call(
        functools.partial(front_kernel, expert_count, capacity),
        out_shape=(
            shape((tokens, model_width), BF16),
            shape((2, expert_count, capacity, model_width), BF16),
            shape((expert_count, capacity, tokens), BF16),
        ),
        in_specs=[vmem] * 5,
        out_specs=(vmem,) * 3,
        compiler_params=pltpu.CompilerParams(vmem_limit_bytes=VMEM_LIMIT),
    )(states[0], upstream, norm_gain, expert_ids[0].T, gate_values[0].T)
    got_rows, got_grads, keys_grad, values_grad, query_grad, w_in, w_out = pl.pallas_call(
        functools.partial(dispatch_kernel, ctx_count, expert_count),
        out_shape=(
            shape((expert_count, capacity, model_width), BF16),
            shape((expert_count, capacity, model_width), BF16),
            shape((key_count, model_width), BF16),
            shape((key_count, model_width), BF16),
            shape((tokens, model_width), BF16),
            shape((hidden, model_width), BF16),
            shape((hidden, model_width), BF16),
        ),
        in_specs=[vmem] * 6,
        out_specs=(vmem,) * 7,
        scratch_shapes=[
            pltpu.VMEM((3, HEADS, tokens), F32),
            pltpu.VMEM((ctx_count - 1, 3, HEADS, tokens), F32),
            pltpu.VMEM((3, HEADS, tokens), F32),
            dma((2, expert_count)),
            dma((2, expert_count, ctx_count - 1)),
            dma((2, expert_count)),
            dma((ctx_count - 1,)),
            dma((ctx_count - 1,)),
        ],
        compiler_params=pltpu.CompilerParams(
            vmem_limit_bytes=VMEM_LIMIT, collective_id=0, has_side_effects=True
        ),
    )(normed, upstream, doc_keys[0], doc_values[0], sends, expert_weights[0])
    slot_rows = expert_count * capacity
    rows = got_rows.reshape(slot_rows, model_width)
    douts = got_grads.reshape(slot_rows, model_width)
    pre = jnp.einsum("sd,hd->sh", rows, w_in, preferred_element_type=jnp.float32)
    activ, pull = jax.vjp(jax.nn.gelu, pre)
    activ_low = activ.astype(jnp.bfloat16)
    act_grad = jnp.einsum("sd,hd->sh", douts, w_out, preferred_element_type=jnp.float32)
    pre_grad = pull(act_grad)[0].astype(jnp.bfloat16)
    block = min(hidden, 128)
    hidden_spec = pl.BlockSpec((slot_rows, block), lambda i: (0, i))
    rows_spec = pl.BlockSpec((slot_rows, model_width), lambda i: (0, 0))
    weights_grad = pl.pallas_call(
        weights_kernel,
        grid=(hidden // block,),
        out_shape=shape((hidden, 2, model_width), BF16),
        in_specs=[hidden_spec, hidden_spec, rows_spec, rows_spec],
        out_specs=pl.BlockSpec((block, 2, model_width), lambda i: (i, 0, 0)),
        compiler_params=pltpu.CompilerParams(vmem_limit_bytes=VMEM_LIMIT),
    )(pre_grad, activ_low, rows, douts)[None]
    partial_rows = jnp.einsum("sh,hd->sd", pre_grad, w_in, preferred_element_type=jnp.float32)
    tiles = model_width // HEAD
    width = HEAD * max(
        (c + 1) * tiles // ctx_count + ((c + 1) * tiles % ctx_count > 0) - c * tiles // ctx_count
        for c in range(ctx_count)
    )
    total_grad = pl.pallas_call(
        functools.partial(return_kernel, ctx_count, expert_count, width),
        out_shape=shape((tokens, model_width), BF16),
        in_specs=[vmem] * 3,
        out_specs=vmem,
        scratch_shapes=[
            pltpu.VMEM((ctx_count - 1, expert_count, capacity, width), BF16),
            pltpu.VMEM((ctx_count - 1, tokens, width), BF16),
            pltpu.VMEM((expert_count, capacity, width), BF16),
            pltpu.VMEM((expert_count, capacity, width), BF16),
            pltpu.VMEM((tokens, width), BF16),
            pltpu.VMEM((ctx_count - 1, tokens, width), BF16),
            dma((ctx_count - 1, expert_count)),
            dma((ctx_count - 1, expert_count)),
            dma((ctx_count - 1,)),
            dma((ctx_count - 1,)),
            dma((expert_count,)),
            dma((expert_count,)),
            dma((ctx_count - 1,)),
            dma((ctx_count - 1,)),
        ],
        compiler_params=pltpu.CompilerParams(
            vmem_limit_bytes=VMEM_LIMIT, collective_id=1, has_side_effects=True
        ),
    )(partial_rows.astype(BF16).reshape(expert_count, capacity, model_width), query_grad, select)
    total_grad = total_grad.astype(F32)
    inputs = states[0].astype(F32)
    inverse = lax.rsqrt(jnp.mean(inputs * inputs, axis=-1, keepdims=True) + EPSILON)
    unit = inputs * inverse
    scaled = total_grad * norm_gain
    states_grad = upstream.astype(jnp.float32) + inverse * (
        scaled - unit * jnp.mean(scaled * unit, axis=-1, keepdims=True)
    )
    return (
        states_grad.astype(jnp.bfloat16)[None],
        keys_grad[None],
        values_grad[None],
        weights_grad,
    )


def solution(mesh):
    return jax.shard_map(
        on_device,
        mesh=mesh,
        in_specs=(
            P("exp", None, None),
            P("exp", None, None),
            P("exp", "ctx", None),
            P("exp", "ctx", None),
            P(),
            P("exp", None, None),
            P("exp", None, None),
            P("exp", "ctx", None, None),
        ),
        out_specs=(
            P("exp", None, None),
            P("exp", "ctx", None),
            P("exp", "ctx", None),
            P("exp", "ctx", None, None),
        ),
        check_vma=False,
    )
```
